32 devices in a mesh: batch: 4 (over y, x), seq: 4 (over z), head: 2 (over core).
Axes of the slice: x: 2, y: 2, z: 4, core: 2. Of those that a mesh axis runs over, the one named last changes fastest.
Arguments:
- hidden: bfloat16 [4, 2048, 1024], P('batch', 'seq', 'head'), may hold values from -6 to 6
- norm_gain: bfloat16 [1024], P('head'), may hold values from 0.099609375 to 1.8984375
- gate_weight: bfloat16 [1024, 2048], P(None, 'head'), may hold values from -0.1875 to 0.1875
- inner_weight: bfloat16 [1024, 2048], P(None, 'head'), may hold values from -0.1875 to 0.1875
- step_weight: bfloat16 [1024, 32], P(None, 'head'), may hold values from -0.375 to 0.375
- maps_weight: bfloat16 [1024, 256], replicated, may hold values from -0.1875 to 0.1875
- inner_kernel: float32 [4, 2048], P(None, 'head'), may hold values from -3 to 3
- inner_bias: float32 [2048], P('head'), may hold values from -1 to 1
- maps_kernel: float32 [4, 256], replicated, may hold values from -3 to 3
- maps_bias: float32 [256], replicated, may hold values from -1 to 1
- step_bias: float32 [32], P('head'), may hold values from -7 to -5
- decay_log: float32 [32], P('head'), may hold values from -5.3 to 1
- skip_gain: float32 [32], P('head'), may hold values from 1 to 4
- gate_gain: float32 [2048], P('head'), may hold values from 0.1 to 1.9
- output_weight: bfloat16 [2048, 1024], P('head'), may hold values from -0.125 to 0.125
- cotangent: bfloat16 [4, 2048, 1024], P('batch', 'seq', 'head'), may hold values from -6 to 6
Outputs:
- output: float32 [4, 2048, 1024], P('batch', 'seq', 'head')
- grad_hidden: float32 [4, 2048, 1024], P('batch', 'seq', 'head')
- grad_norm_gain: float32 [1024], P('head')
- grad_gate_weight: float32 [1024, 2048], P(None, 'head')
- grad_inner_weight: float32 [1024, 2048], P(None, 'head')
- grad_step_weight: float32 [1024, 32], P(None, 'head')
- grad_maps_weight: float32 [1024, 256], replicated
- grad_inner_kernel: float32 [4, 2048], P(None, 'head')
- grad_inner_bias: float32 [2048], P('head')
- grad_maps_kernel: float32 [4, 256], replicated
- grad_maps_bias: float32 [256], replicated
- grad_step_bias: float32 [32], P('head')
- grad_decay_log: float32 [32], P('head')
- grad_skip_gain: float32 [32], P('head')
- grad_gate_gain: float32 [2048], P('head')
- grad_output_weight: float32 [2048, 1024], P('head')
The draws below stay inside these ranges and needn't reach their ends.
All inputs are finite; a program needn't handle non-finite values.
Results may differ from the reference program's by a relative error of at most 0.0089.
Values may be sent and summed in bfloat16 or wider, within the bound.
A program may use at most 192 MiB of HBM per device.

```python
import jax
import jax.numpy as jnp
from jax import lax

D = 1024
HEADS = 32
HEADDIM = 64
STATE = 128
CONV = 4
GROUP = 256
DI = 2048
SEQS = 4
LEN = 2048


def shard_levels(stream_key, extent, cuts, low, top_value):
    level = 1.0
    for dim, parts in cuts:
        heights = jax.random.uniform(jax.random.fold_in(jax.random.fold_in(stream_key, 6), dim), (parts,), jnp.float32, low / len(cuts), top_value / len(cuts))
        level = level * jnp.repeat(jnp.exp(heights), extent[dim] // parts).reshape((-1,) + (1,) * (len(extent) - 1 - dim))
    return level


def scatter_about(own_key, shape, width, limit, split=(), kind=jnp.bfloat16):
    values = jax.random.normal(own_key, shape, jnp.float32) * width
    if len(split) > 0:
        values = shard_levels(own_key, shape, split, -0.22, 0.18) * values
    return jnp.clip(values, min=-limit, max=limit).astype(kind)


def setup_inputs(seed: int = 0) -> dict:
    streams_of = jax.random.split(jax.random.key(seed), 17)
    hidden = scatter_about(streams_of[0], (SEQS, LEN, D), 1.0, 6.0, ((0, 4), (1, 4), (2, 2)))
    norm_gain = jnp.clip(1.0 + 0.18 * jax.random.normal(streams_of[1], (D,), jnp.float32), 0.099609375, 1.8984375).astype(jnp.bfloat16)
    gate_weight = scatter_about(streams_of[2], (D, DI), D ** -0.5, 0.1875, ((1, 2),))
    inner_weight = scatter_about(streams_of[3], (D, DI), D ** -0.5, 0.1875, ((1, 2),))
    step_weight = scatter_about(streams_of[4], (D, HEADS), (D // 4) ** -0.5, 0.375, ((1, 2),))
    maps_weight = scatter_about(streams_of[5], (D, 2 * STATE), D ** -0.5, 0.1875)
    inner_kernel = scatter_about(streams_of[6], (CONV, DI), CONV ** -0.5, 3.0, ((1, 2),), jnp.float32)
    inner_bias = jnp.clip(jax.random.uniform(streams_of[7], (DI,), jnp.float32, -1.0, 1.0) * shard_levels(streams_of[7], (DI,), ((0, 2),), -0.4, 0.0), -1.0, 1.0)
    maps_kernel = scatter_about(streams_of[8], (CONV, 2 * STATE), CONV ** -0.5, 3.0, (), jnp.float32)
    maps_bias = jnp.clip(jax.random.uniform(streams_of[9], (2 * STATE,), jnp.float32, -1.0, 1.0), -1.0, 1.0)
    step_bias = jnp.clip(-7.0 + 2.0 * jax.random.uniform(streams_of[10], (HEADS,), jnp.float32) ** shard_levels(streams_of[10], (HEADS,), ((0, 2),), -0.2, 0.2), -7.0, -5.0)
    decay_log = jnp.clip(-5.3 + 6.3 * jax.random.uniform(streams_of[11], (HEADS,), jnp.float32) ** shard_levels(streams_of[11], (HEADS,), ((0, 2),), -0.2, 0.2), -5.3, 1.0)
    skip_gain = jnp.clip(1.0 + 3.0 * jax.random.uniform(streams_of[12], (HEADS,), jnp.float32) ** shard_levels(streams_of[12], (HEADS,), ((0, 2),), -0.2, 0.2), 1.0, 4.0)
    gate_gain = jnp.clip(1.0 + 0.18 * jax.random.normal(streams_of[13], (DI,), jnp.float32), 0.1, 1.9)
    output_weight = scatter_about(streams_of[14], (DI, D), DI ** -0.5, 0.125, ((0, 2),))
    cotangent = scatter_about(streams_of[15], (SEQS, LEN, D), 1.0, 6.0, ((0, 4), (1, 4), (2, 2)))
    return {"hidden": hidden, "norm_gain": norm_gain, "gate_weight": gate_weight, "inner_weight": inner_weight, "step_weight": step_weight, "maps_weight": maps_weight, "inner_kernel": inner_kernel, "inner_bias": inner_bias, "maps_kernel": maps_kernel, "maps_bias": maps_bias, "step_bias": step_bias, "decay_log": decay_log, "skip_gain": skip_gain, "gate_gain": gate_gain, "output_weight": output_weight, "cotangent": cotangent}


HIGH = lax.Precision.HIGHEST
EPSILON = 1e-05

def silu_slope(values):
    sigmoid = jax.nn.sigmoid(values)
    return sigmoid * (1.0 + values * (1.0 - sigmoid))

def ssd_blocks(inner_act, write_map, read_map, step_size, decay_rates, initial):
    length, heads, headdim = inner_act.shape
    blocks_count = length // GROUP
    inner_blocks = inner_act.reshape(blocks_count, GROUP, heads, headdim)
    write_blocks = write_map.reshape(blocks_count, GROUP, write_map.shape[-1])
    read_blocks = read_map.reshape(blocks_count, GROUP, read_map.shape[-1])
    step_blocks = step_size.reshape(blocks_count, GROUP, heads)
    causal = (jnp.arange(GROUP)[:, None] >= jnp.arange(GROUP)[None, :])[:, :, None]

    def advance(state_in, pieces):
        inner_part, write_part, read_part, step_part = pieces
        cumlog = jnp.cumsum(step_part * decay_rates[None, :], axis=0)
        spread = jnp.where(causal, cumlog[:, None, :] - cumlog[None, :, :], 0.0)
        decays = jnp.where(causal, jnp.exp(spread), 0.0)
        scores = jnp.dot(read_part, write_part.T, precision=HIGH)
        weighted = inner_part * step_part[:, :, None]
        within = jnp.einsum('tsh,shp->thp', decays * scores[:, :, None], weighted, precision=HIGH)
        carried = jnp.einsum('tn,hpn->thp', read_part, state_in, precision=HIGH)
        result = within + jnp.exp(cumlog)[:, :, None] * carried
        remain = jnp.exp(cumlog[-1][None, :] - cumlog)
        fresh = jnp.einsum('shp,sn->hpn', weighted * remain[:, :, None], write_part, precision=HIGH)
        state_out = jnp.exp(cumlog[-1])[:, None, None] * state_in + fresh
        return (state_out, result)
    final, outputs = lax.scan(advance, initial, (inner_blocks, write_blocks, read_blocks, step_blocks))
    return (outputs.reshape(length, heads, headdim), final)

def conv_apply(padded, kernel, bias_row, length):
    summed = bias_row
    for offset in range(kernel.shape[0]):
        summed = summed + kernel[offset] * padded[..., offset:offset + length, :]
    return summed

def conv_grads(padded, extended, grad_out, kernel, length):
    leading = tuple(range(grad_out.ndim - 1))
    grad_kernel = jnp.stack([lax.optimization_barrier(jnp.sum(grad_out * padded[..., offset:offset + length, :], axis=leading)) for offset in range(kernel.shape[0])])
    grad_bias = lax.optimization_barrier(jnp.sum(grad_out, axis=leading))
    width_less = kernel.shape[0] - 1
    grad_input = jnp.zeros_like(grad_out)
    for offset in range(kernel.shape[0]):
        begin_at = width_less - offset
        grad_input = grad_input + kernel[offset] * extended[..., begin_at:begin_at + length, :]
    return (grad_input, grad_kernel, grad_bias)

def one_sequence(hidden, cotangent, norm_gain, gate_weight, inner_weight, step_weight, maps_weight, inner_kernel, inner_bias, maps_kernel, maps_bias, step_bias, decay_log, skip_gain, gate_gain, output_weight):
    length = hidden.shape[0]
    residual = hidden.astype(jnp.float32)
    inverse = lax.rsqrt(lax.optimization_barrier(jnp.mean(residual * residual, axis=-1, keepdims=True)) + EPSILON)
    normal = residual * inverse
    normed = (normal * norm_gain.astype(jnp.float32)).astype(jnp.bfloat16)
    gate_pre = jnp.dot(normed, gate_weight, preferred_element_type=jnp.float32)
    inner_pre = jnp.dot(normed, inner_weight, preferred_element_type=jnp.float32)
    maps_pre = jnp.dot(normed, maps_weight, preferred_element_type=jnp.float32)
    step_pre = jnp.dot(normed, step_weight, preferred_element_type=jnp.float32)
    inner_pad = jnp.concatenate([jnp.zeros((CONV - 1, inner_pre.shape[1]), jnp.float32), inner_pre], axis=0)
    maps_pad = jnp.concatenate([jnp.zeros((CONV - 1, maps_pre.shape[1]), jnp.float32), maps_pre], axis=0)
    inner_conv = conv_apply(inner_pad, inner_kernel, inner_bias, length)
    maps_conv = conv_apply(maps_pad, maps_kernel, maps_bias, length)
    inner_act = jax.nn.silu(inner_conv)
    maps_act = jax.nn.silu(maps_conv)
    write_map = maps_act[:, :STATE]
    read_map = maps_act[:, STATE:]
    step_size = jax.nn.softplus(step_pre + step_bias)
    decay_rates = -jnp.exp(decay_log)
    inner_heads = inner_act.reshape(length, HEADS, HEADDIM)
    zero_state = jnp.zeros((HEADS, HEADDIM, STATE), jnp.float32)

    def scan_only(inner_arg, write_arg, read_arg, step_arg, rate_arg):
        return ssd_blocks(inner_arg, write_arg, read_arg, step_arg, rate_arg, zero_state)[0]
    scanned, scan_back = jax.vjp(scan_only, inner_heads, write_map, read_map, step_size, decay_rates)
    mixed_out = scanned + skip_gain[None, :, None] * inner_heads
    mixed_flat = mixed_out.reshape(length, DI)
    gate_act = jax.nn.silu(gate_pre)
    gated_val = mixed_flat * gate_act
    scale_back = lax.rsqrt(lax.optimization_barrier(jnp.mean(gated_val * gated_val, axis=-1, keepdims=True)) + EPSILON)
    gated_norm = (gated_val * scale_back * gate_gain).astype(jnp.bfloat16)
    branch = jnp.dot(gated_norm, output_weight, preferred_element_type=jnp.float32)
    output = residual + branch
    grad_output_weight = jnp.dot(gated_norm.T, cotangent, preferred_element_type=jnp.float32)
    grad_norm_out = jnp.dot(cotangent, output_weight.T, preferred_element_type=jnp.float32)
    grad_gate_gain = lax.optimization_barrier(jnp.sum(grad_norm_out * gated_val * scale_back, axis=0))
    grad_scaled = grad_norm_out * gate_gain
    row_mean = lax.optimization_barrier(jnp.mean(grad_scaled * gated_val, axis=-1, keepdims=True))
    grad_gated = scale_back * (grad_scaled - gated_val * scale_back * scale_back * row_mean)
    grad_mixed = (grad_gated * gate_act).reshape(length, HEADS, HEADDIM)
    grad_gate_pre = grad_gated * mixed_flat * silu_slope(gate_pre)
    grad_skip_gain = lax.optimization_barrier(jnp.sum(grad_mixed * inner_heads, axis=(0, 2)))
    grad_inner_heads, grad_write, grad_read, grad_step, grad_rates = scan_back(grad_mixed)
    grad_inner = (grad_inner_heads + skip_gain[None, :, None] * grad_mixed).reshape(length, DI)
    grad_maps = jnp.concatenate([grad_write, grad_read], axis=1)
    grad_inner_conv = grad_inner * silu_slope(inner_conv)
    grad_maps_conv = grad_maps * silu_slope(maps_conv)
    grad_step_pre = grad_step * jax.nn.sigmoid(step_pre + step_bias)
    grad_step_bias = lax.optimization_barrier(jnp.sum(grad_step_pre, axis=0))
    grad_decay_log = grad_rates * decay_rates
    inner_ext = jnp.concatenate([grad_inner_conv, jnp.zeros((CONV - 1, grad_inner_conv.shape[1]), jnp.float32)], axis=0)
    maps_ext = jnp.concatenate([grad_maps_conv, jnp.zeros((CONV - 1, grad_maps_conv.shape[1]), jnp.float32)], axis=0)
    grad_inner_pre, grad_inner_kernel, grad_inner_bias = conv_grads(inner_pad, inner_ext, grad_inner_conv, inner_kernel, length)
    grad_maps_pre, grad_maps_kernel, grad_maps_bias = conv_grads(maps_pad, maps_ext, grad_maps_conv, maps_kernel, length)
    gate_round = grad_gate_pre.astype(jnp.bfloat16)
    inner_round = grad_inner_pre.astype(jnp.bfloat16)
    maps_round = grad_maps_pre.astype(jnp.bfloat16)
    step_round = grad_step_pre.astype(jnp.bfloat16)
    grad_gate_weight = jnp.dot(normed.T, gate_round, preferred_element_type=jnp.float32)
    grad_inner_weight = jnp.dot(normed.T, inner_round, preferred_element_type=jnp.float32)
    grad_maps_weight = jnp.dot(normed.T, maps_round, preferred_element_type=jnp.float32)
    grad_step_weight = jnp.dot(normed.T, step_round, preferred_element_type=jnp.float32)
    grad_normed = jnp.dot(gate_round, gate_weight.T, preferred_element_type=jnp.float32)
    grad_normed = grad_normed + jnp.dot(inner_round, inner_weight.T, preferred_element_type=jnp.float32)
    grad_normed = grad_normed + jnp.dot(step_round, step_weight.T, preferred_element_type=jnp.float32)
    grad_normed = grad_normed + jnp.dot(maps_round, maps_weight.T, preferred_element_type=jnp.float32)
    grad_norm_gain = lax.optimization_barrier(jnp.sum(grad_normed * normal, axis=0))
    grad_normal = grad_normed * norm_gain.astype(jnp.float32)
    grad_hidden = inverse * (grad_normal - normal * lax.optimization_barrier(jnp.mean(grad_normal * normal, axis=-1, keepdims=True))) + cotangent.astype(jnp.float32)
    grads = (grad_norm_gain, grad_gate_weight, grad_inner_weight, grad_step_weight, grad_maps_weight, grad_inner_kernel, grad_inner_bias, grad_maps_kernel, grad_maps_bias, grad_step_bias, grad_decay_log, grad_skip_gain, grad_gate_gain, grad_output_weight)
    return (output, grad_hidden, grads)

def reference(hidden, norm_gain, gate_weight, inner_weight, step_weight, maps_weight, inner_kernel, inner_bias, maps_kernel, maps_bias, step_bias, decay_log, skip_gain, gate_gain, output_weight, cotangent):
    params = (norm_gain, gate_weight, inner_weight, step_weight, maps_weight, inner_kernel, inner_bias, maps_kernel, maps_bias, step_bias, decay_log, skip_gain, gate_gain, output_weight)
    start = tuple((jnp.zeros(item.shape, jnp.float32) for item in params))

    def per_sequence(totals, rows):
        output, grad_hidden, grads = one_sequence(rows[0], rows[1], norm_gain, gate_weight, inner_weight, step_weight, maps_weight, inner_kernel, inner_bias, maps_kernel, maps_bias, step_bias, decay_log, skip_gain, gate_gain, output_weight)
        return (jax.tree.map(jnp.add, totals, grads), (output, grad_hidden))
    totals, stacked = lax.scan(per_sequence, start, (hidden, cotangent))
    return (stacked[0], stacked[1], totals[0], totals[1], totals[2], totals[3], totals[4], totals[5], totals[6], totals[7], totals[8], totals[9], totals[10], totals[11], totals[12], totals[13])
```

```python
import jax
import jax.numpy as jnp
from jax import lax
from jax.experimental import pallas as pl
from jax.experimental.pallas import tpu as pltpu
from jax.sharding import PartitionSpec as P

HEADDIM = 64
BLK = 256
PAD = 8
EPSILON = 1e-05
HIGH = lax.Precision.HIGHEST
F32 = jnp.float32
BF16 = jnp.bfloat16
FAR = -1e30


def dot(a, b):
    return jnp.dot(a, b, preferred_element_type=F32)


def dot_t(a, b):
    return lax.dot_general(a, b, (((1,), (1,)), ((), ())), preferred_element_type=F32)


def t_dot(a, b):
    return lax.dot_general(a, b, (((0,), (0,)), ((), ())), preferred_element_type=F32)


def fine(a, b, dims):
    return lax.dot_general(a, b, ((dims[:1], dims[1:]), ((), ())), precision=HIGH, preferred_element_type=F32)


def sigmoid(v):
    return 1.0 / (1.0 + jnp.exp(-v))


def silu_slope(v):
    s = sigmoid(v)
    return s * (1.0 + v * (1.0 - s))


def first_half(shape):
    return lax.broadcasted_iota(jnp.int32, shape, 1) < HEADDIM


def lanes(pair, width):
    return jnp.where(first_half((pair.shape[0], width)), pair[:, 0:1], pair[:, 1:2])


def put_pair(ref, values):
    mask = first_half(values.shape)
    ref[0, :, 0:1] = jnp.sum(jnp.where(mask, values, 0.0), axis=1, keepdims=True)
    ref[0, :, 1:2] = jnp.sum(jnp.where(mask, 0.0, values), axis=1, keepdims=True)


def conv_rows(ext_ref, kern_ref, bias_ref, length):
    taps = kern_ref.shape[0]
    total = bias_ref[...]
    for k in range(taps):
        begin = PAD - (taps - 1) + k
        total = total + kern_ref[k : k + 1, :] * ext_ref[begin : begin + length, :]
    return total


def maps_conv_kernel(ext_ref, kern_ref, bias_ref, conv_ref, act_ref):
    conv = conv_rows(ext_ref, kern_ref, bias_ref, conv_ref.shape[0])
    conv_ref[...] = conv
    act_ref[...] = conv * sigmoid(conv)


def enter_kernel(ext_ref, kern_ref, bias_ref, dt_ref, cum_ref, b_ref, conv_ref, act_ref, xdt_ref, state_ref):
    length, width = conv_ref.shape
    conv = conv_rows(ext_ref, kern_ref, bias_ref, length)
    act = conv * sigmoid(conv)
    conv_ref[...] = conv
    act_ref[...] = act
    xdt = act * lanes(dt_ref[0], width)
    xdt_ref[...] = xdt
    cum = cum_ref[0]
    remain = jnp.exp(cum[length - 1 : length, :] - cum)
    state_ref[...] = fine(b_ref[...], xdt * lanes(remain, width), (0, 0))


def within_kernel(c_ref, b_ref, cum_ref, cumt_ref, xdt_ref, y_ref, g_ref):
    length, width = y_ref.shape

    @pl.when(pl.program_id(0) == 0)
    def _():
        g_ref[...] = fine(c_ref[...], b_ref[...], (1, 1))

    cum = cum_ref[0]
    cumt = cumt_ref[0]
    for r in range(0, length, BLK):
        w = r + BLK
        causal = (lax.broadcasted_iota(jnp.int32, (BLK, w), 0) + r) >= lax.broadcasted_iota(
            jnp.int32, (BLK, w), 1
        )
        g = g_ref[r : r + BLK, :w]
        x = xdt_ref[:w, :].astype(BF16)
        parts = []
        for h in range(2):
            diff = cum[r : r + BLK, h : h + 1] - cumt[h : h + 1, :w]
            m = jnp.exp(jnp.where(causal, diff, FAR))
            parts.append(dot((m * g).astype(BF16), x))
        y_ref[r : r + BLK, :] = jnp.where(first_half((BLK, width)), parts[0], parts[1])


def mix_kernel(y_ref, act_ref, gate_ref, gno_ref, c_ref, s_ref, cum_ref, skip_ref, gain_ref, mixed_ref, rows_ref, sq_ref, dt_ref):
    length, width = y_ref.shape
    carried = fine(c_ref[...], s_ref[...], (1, 0)) * lanes(jnp.exp(cum_ref[0]), width)
    mixed = y_ref[...] + carried + skip_ref[...] * act_ref[...]
    mixed_ref[...] = mixed
    gate = gate_ref[...]
    gated = mixed * (gate * sigmoid(gate))
    first = pl.program_id(0) == 0
    square = gated * gated
    inner = gno_ref[...] * gain_ref[...] * gated

    @pl.when(first)
    def _():
        sq_ref[...] = square
        dt_ref[...] = inner

    @pl.when(jnp.logical_not(first))
    def _():
        sq_ref[...] += square
        dt_ref[...] += inner

    @pl.when(pl.program_id(0) == pl.num_programs(0) - 1)
    def _():
        rows_ref[:, 0:1] = jnp.sum(sq_ref[...], axis=1, keepdims=True)
        rows_ref[:, 1:2] = jnp.sum(dt_ref[...], axis=1, keepdims=True)


def gate_back_kernel(mixed_ref, gate_ref, gno_ref, act_ref, gain_ref, c_ref, s_ref, cum_ref, rows_ref,
                     norm_ref, dy_ref, ground_ref, from_ref, dc_ref, ggain_ref, gskip_ref, plus_ref):
    length, width = mixed_ref.shape
    scale = rows_ref[:, 0:1]
    coef = rows_ref[:, 1:2]
    gate = gate_ref[...]
    sig = sigmoid(gate)
    gate_act = gate * sig
    slope = sig * (1.0 + gate * (1.0 - sig))
    mixed = mixed_ref[...]
    gain = gain_ref[...]
    gno = gno_ref[...]
    gated = mixed * gate_act
    scaled = gated * scale
    norm_ref[...] = (scaled * gain).astype(BF16)
    ggain_ref[...] = jnp.sum(gno * scaled, axis=0, keepdims=True)
    grad_gated = scale * (gno * gain) - gated * coef
    dy = grad_gated * gate_act
    dy_ref[...] = dy
    ground_ref[...] = (grad_gated * mixed * slope).astype(BF16)
    gskip_ref[...] = jnp.sum(dy * act_ref[...], axis=0, keepdims=True)
    dye = dy * lanes(jnp.exp(cum_ref[0]), width)
    c = c_ref[...]
    s = s_ref[...]
    from_ref[...] = fine(c, dye, (0, 0))
    put_pair(plus_ref, dye * fine(c, s, (1, 0)))
    dc = fine(dye, s, (1, 1))
    first = pl.program_id(0) == 0

    @pl.when(first)
    def _():
        dc_ref[...] = dc

    @pl.when(jnp.logical_not(first))
    def _():
        dc_ref[...] += dc


def within_back_kernel(c_ref, b_ref, cum_ref, cumt_ref, xdt_ref, dy_ref, dx_ref, plus_ref, minus_ref, db_ref, dc_ref, g_ref, dg_ref):
    length, width = dx_ref.shape

    @pl.when(pl.program_id(0) == 0)
    def _():
        g_ref[...] = fine(b_ref[...], c_ref[...], (1, 1))
        dg_ref[...] = jnp.zeros_like(dg_ref)

    cum = cum_ref[0]
    cumt = cumt_ref[0]
    plus_ref[...] = jnp.zeros_like(plus_ref)
    for r in range(0, length, BLK):
        w = length - r
        causal = lax.broadcasted_iota(jnp.int32, (BLK, w), 0) <= lax.broadcasted_iota(
            jnp.int32, (BLK, w), 1
        )
        g = g_ref[r : r + BLK, r:]
        x = xdt_ref[r : r + BLK, :]
        dy_fine = dy_ref[r:, :]
        dy = dy_fine.astype(BF16)
        half = first_half((BLK, width))
        parts = []
        dg = None
        for h in range(2):
            diff = cumt[h : h + 1, r:] - cum[r : r + BLK, h : h + 1]
            m = jnp.exp(jnp.where(causal, diff, FAR))
            xh = jnp.where(half == (h == 0), x, jnp.zeros_like(x))
            mq = m * fine(xh, dy_fine, (1, 1))
            dg = mq if dg is None else dg + mq
            d = mq * g
            parts.append(dot((m * g).astype(BF16), dy))
            minus_ref[0, r : r + BLK, h : h + 1] = jnp.sum(d, axis=1, keepdims=True)
            plus_ref[0, h : h + 1, r:] += jnp.sum(d, axis=0, keepdims=True)
        dx_ref[r : r + BLK, :] = jnp.where(half, parts[0], parts[1])
        dg_ref[r : r + BLK, r:] += dg

    @pl.when(pl.program_id(0) == pl.num_programs(0) - 1)
    def _():
        dg = dg_ref[...]
        db_ref[...] = fine(dg, c_ref[...], (1, 0))
        dc_ref[...] = fine(dg, b_ref[...], (0, 0))


def leave_back_kernel(dx_ref, ds_ref, b_ref, act_ref, dy_ref, dt_ref, cum_ref, conv_ref, skip_ref, gic_ref, gdt_ref, minus_ref, db_ref):
    length, width = dx_ref.shape
    cum = cum_ref[0]
    remain = lanes(jnp.exp(cum[length - 1 : length, :] - cum), width)
    ds = ds_ref[...]
    bs = fine(b_ref[...], ds, (1, 0)) * remain
    dxd = dx_ref[...] + bs
    act = act_ref[...]
    dt = lanes(dt_ref[0], width)
    xdt = act * dt
    grad_act = dt * dxd + skip_ref[...] * dy_ref[...]
    gic_ref[...] = grad_act * silu_slope(conv_ref[...])
    put_pair(gdt_ref, dxd * act)
    put_pair(minus_ref, xdt * bs)
    db = fine(xdt * remain, ds, (1, 1))
    first = pl.program_id(0) == 0

    @pl.when(first)
    def _():
        db_ref[...] = db

    @pl.when(jnp.logical_not(first))
    def _():
        db_ref[...] += db


def conv_back_kernel(gic_ref, next_ref, ext_ref, kern_ref, round_ref, gkern_ref, gbias_ref, buf_ref):
    length = gic_ref.shape[0]
    taps = kern_ref.shape[0]
    gic = gic_ref[...]
    buf_ref[:length, :] = gic
    buf_ref[length:, :] = next_ref[...]
    total = None
    for k in range(taps):
        at = taps - 1 - k
        term = kern_ref[k : k + 1, :] * buf_ref[at : at + length, :]
        total = term if total is None else total + term
        begin = PAD - (taps - 1) + k
        gkern_ref[k : k + 1, :] = jnp.sum(gic * ext_ref[begin : begin + length, :], axis=0, keepdims=True)
    round_ref[...] = total.astype(BF16)
    gbias_ref[...] = jnp.sum(gic, axis=0, keepdims=True)


def col(rows, width):
    return pl.BlockSpec((rows, width), lambda i: (0, i))


def full(rows, width):
    return pl.BlockSpec((rows, width), lambda i: (0, 0))


def lead(rows, width):
    return pl.BlockSpec((1, rows, width), lambda i: (i, 0, 0))


def out(shape, dtype=F32):
    return jax.ShapeDtypeStruct(shape, dtype)


def call(kernel, steps, ins, outs, shapes, scratch=()):
    return pl.pallas_call(
        kernel,
        grid=(steps,),
        in_specs=ins,
        out_specs=outs,
        out_shape=shapes,
        scratch_shapes=list(scratch),
        compiler_params=pltpu.CompilerParams(
            dimension_semantics=("arbitrary",), vmem_limit_bytes=48 * 1024 * 1024
        ),
    )


def swap(array):
    count = lax.axis_size("head")
    return lax.ppermute(array, "head", [(i, (i + 1) % count) for i in range(count)])


def shifted(array, by):
    count = lax.axis_size("seq")
    pairs = [(i, i + by) for i in range(count) if 0 <= i + by < count]
    return lax.ppermute(array, "seq", pairs)


def joined(own, other, axis):
    first = lax.axis_index("head") == 0
    low = jnp.where(first, own, other)
    high = jnp.where(first, other, own)
    return jnp.concatenate([low, high], axis=axis)


def entering(state, log_totals, repeat, reverse):
    count, index = lax.axis_size("seq"), lax.axis_index("seq")
    total = None
    log_scale = jnp.zeros_like(log_totals[0])
    for by in range(1, count):
        part = shifted(state, -by if reverse else by).astype(F32)
        term = part * repeat(jnp.exp(log_scale))
        total = term if total is None else total + term
        at = jnp.clip(index + by if reverse else index - by, 0, count - 1)
        log_scale = log_scale + lax.dynamic_index_in_dim(log_totals, at, 0, keepdims=False)
    return total


def on_device(hidden, norm_gain, gate_weight, inner_weight, step_weight, maps_weight, inner_kernel, inner_bias,
              maps_kernel, maps_bias, step_bias, decay_log, skip_gain, gate_gain, output_weight, cotangent):
    seq_count, length, local_width = hidden.shape
    width_all = gate_weight.shape[0]
    inner = gate_weight.shape[1]
    inner_all = inner * lax.axis_size("head")
    heads = step_weight.shape[1]
    state = maps_weight.shape[1] // 2
    pairs = heads // 2
    pw = 2 * HEADDIM
    taps = inner_kernel.shape[0]
    own_h = hidden.reshape(length, local_width)
    own_c = cotangent.reshape(length, local_width)
    heads_n, seq_n = lax.axis_size("head"), lax.axis_size("seq")
    tail = own_h[length - PAD :, :]
    perm = [(s * heads_n + h, (s + 1) * heads_n + (1 - h)) for s in range(seq_n - 1) for h in range(heads_n)]
    tail_own = shifted(tail, 1)
    tail_other = lax.ppermute(tail, ("seq", "head"), perm)
    other_h, other_gain, other_c = swap(own_h), swap(norm_gain), swap(own_c)
    ext_h = joined(
        jnp.concatenate([tail_own, own_h], axis=0), jnp.concatenate([tail_other, other_h], axis=0), 1
    )
    gain = joined(norm_gain, other_gain, 0).astype(F32)
    cot = joined(own_c, other_c, 1)
    residual = ext_h.astype(F32)
    inverse_ext = lax.rsqrt(jnp.mean(residual * residual, axis=-1, keepdims=True) + EPSILON)
    normed_ext = (residual * inverse_ext * gain).astype(BF16)
    normed = normed_ext[PAD:]
    inverse = inverse_ext[PAD:]
    step_pre = dot(normed, step_weight) + step_bias
    maps_ext = dot(normed_ext, maps_weight)
    inner_ext = dot(normed_ext, inner_weight)
    dt = jax.nn.softplus(step_pre)
    rates = -jnp.exp(decay_log)
    lower = (jnp.arange(length)[:, None] >= jnp.arange(length)[None, :]).astype(F32)
    cum = jnp.dot(lower, dt * rates, precision=HIGH)
    log_totals = lax.all_gather(cum[length - 1], "seq")
    pair_of = lambda v: v.reshape(length, pairs, 2).transpose(1, 0, 2)
    unpair = lambda v: v.transpose(1, 0, 2).reshape(length, heads)
    repeat = lambda v: jnp.repeat(v, HEADDIM)[None, :]
    dt_p, cum_p = pair_of(dt), pair_of(cum)
    cumt_p = cum.T.reshape(pairs, 2, length)
    skip_row = repeat(skip_gain)
    gain_row = gate_gain[None, :]

    maps_conv, maps_act = call(
        maps_conv_kernel, 2,
        [col(length + PAD, state), col(taps, state), col(1, state)],
        [col(length, state), col(length, state)],
        [out((length, 2 * state)), out((length, 2 * state))],
    )(maps_ext, maps_kernel, maps_bias[None, :])
    write_map, read_map = maps_act[:, :state], maps_act[:, state:]
    maps_full = full(length, state)
    inner_conv, inner_act, xdt, local_state = call(
        enter_kernel, pairs,
        [col(length + PAD, pw), col(taps, pw), col(1, pw), lead(length, 2), lead(length, 2), maps_full],
        [col(length, pw), col(length, pw), col(length, pw), col(state, pw)],
        [out((length, inner)), out((length, inner)), out((length, inner)), out((state, inner))],
    )(inner_ext, inner_kernel, inner_bias[None, :], dt_p, cum_p, write_map)
    state_in = entering(local_state.astype(BF16), log_totals, repeat, False)
    gate_pre = dot(normed, gate_weight)
    grad_norm_out = dot_t(cot, output_weight)
    within = call(
        within_kernel, pairs,
        [maps_full, maps_full, lead(length, 2), lead(2, length), col(length, pw)],
        col(length, pw), out((length, inner)),
        [pltpu.VMEM((length, length), F32)],
    )(read_map, write_map, cum_p, cumt_p, xdt)
    mixed, row_sums = call(
        mix_kernel, pairs,
        [col(length, pw)] * 4 + [maps_full, col(state, pw), lead(length, 2), col(1, pw), col(1, pw)],
        [col(length, pw), full(length, 2)],
        [out((length, inner)), out((length, 2))],
        [pltpu.VMEM((length, pw), F32), pltpu.VMEM((length, pw), F32)],
    )(within, inner_act, gate_pre, grad_norm_out, read_map, state_in, cum_p, skip_row, gain_row)
    row_sums = row_sums + swap(row_sums)
    scale = lax.rsqrt(row_sums[:, 0:1] / inner_all + EPSILON)
    coef = scale * scale * scale * (row_sums[:, 1:2] / inner_all)
    scales = jnp.concatenate([scale, coef], axis=1)
    gated_norm, grad_mixed, gate_round, from_here, grad_read_in, gate_gain_row, skip_lanes, plus_in = call(
        gate_back_kernel, pairs,
        [col(length, pw)] * 4 + [col(1, pw), maps_full, col(state, pw), lead(length, 2), full(length, 2)],
        [col(length, pw)] * 3 + [col(state, pw), maps_full, col(1, pw), col(1, pw), lead(length, 2)],
        [out((length, inner), BF16), out((length, inner)), out((length, inner), BF16), out((state, inner)),
         out((length, state)), out((1, inner)), out((1, inner)), out((pairs, length, 2))],
    )(mixed, gate_pre, grad_norm_out, inner_act, gain_row, read_map, state_in, cum_p, scales)
    state_grad = entering(from_here.astype(BF16), log_totals, repeat, True)
    reduce = lambda v: lax.psum(v, ("batch", "seq"))
    out_sum = reduce(t_dot(gated_norm, cot).astype(BF16))
    gate_part, out_sum = lax.optimization_barrier((t_dot(normed, gate_round).astype(BF16), out_sum))
    gate_sum = reduce(gate_part)
    grad_output_weight = out_sum.astype(F32)
    dx, plus_w, minus_w, grad_write, grad_read = call(
        within_back_kernel, pairs,
        [maps_full, maps_full, lead(length, 2), lead(2, length), col(length, pw), col(length, pw)],
        [col(length, pw), lead(2, length), lead(length, 2), maps_full, maps_full],
        [out((length, inner)), out((pairs, 2, length)), out((pairs, length, 2)),
         out((length, state)), out((length, state))],
        [pltpu.VMEM((length, length), F32), pltpu.VMEM((length, length), F32)],
    )(read_map, write_map, cum_p, cumt_p, xdt, grad_mixed)
    grad_inner_conv, grad_dt, minus_in, grad_write_in = call(
        leave_back_kernel, pairs,
        [col(length, pw), col(state, pw), maps_full, col(length, pw), col(length, pw), lead(length, 2),
         lead(length, 2), col(length, pw), col(1, pw)],
        [col(length, pw), lead(length, 2), lead(length, 2), maps_full],
        [out((length, inner)), out((pairs, length, 2)), out((pairs, length, 2)), out((length, state))],
    )(dx, state_grad, write_map, inner_act, grad_mixed, dt_p, cum_p, inner_conv, skip_row)
    grad_maps = jnp.concatenate([grad_write + grad_write_in, grad_read + grad_read_in], axis=1)
    grad_maps = grad_maps + swap(grad_maps)
    grad_maps_conv = grad_maps * silu_slope(maps_conv)
    next_inner = shifted(grad_inner_conv[:PAD], -1)
    next_maps = shifted(grad_maps_conv[:PAD], -1)

    def conv_back(gic, nxt, ext, kern, width):
        total = gic.shape[1]
        return call(
            conv_back_kernel, total // width,
            [col(length, width), col(PAD, width), col(length + PAD, width), col(taps, width)],
            [col(length, width), col(taps, width), col(1, width)],
            [out((length, total), BF16), out((taps, total)), out((1, total))],
            [pltpu.VMEM((length + PAD, width), F32)],
        )(gic, nxt, ext, kern)

    inner_round, grad_inner_kernel, grad_inner_bias = conv_back(grad_inner_conv, next_inner, inner_ext, inner_kernel, pw)
    maps_round, grad_maps_kernel, grad_maps_bias = conv_back(grad_maps_conv, next_maps, maps_ext, maps_kernel, state)

    state_out = jnp.exp(repeat(cum[length - 1])) * state_in + local_state
    at_end = jnp.sum(jnp.sum(state_grad * state_out, axis=0).reshape(heads, HEADDIM), axis=1)
    grad_cum = plus_w.reshape(heads, length).T - unpair(minus_w - plus_in + minus_in)
    grad_log = jnp.dot(lower.T, grad_cum, precision=HIGH) + at_end
    grad_step_pre = (unpair(grad_dt) + grad_log * rates) * jax.nn.sigmoid(step_pre)
    grad_decay_log = jnp.sum(grad_log * dt, axis=0) * rates
    grad_step_bias = jnp.sum(grad_step_pre, axis=0)
    grad_skip_gain = jnp.sum(skip_lanes.reshape(heads, HEADDIM), axis=1)
    step_round = grad_step_pre.astype(BF16)

    grad_inner_weight = t_dot(normed, inner_round)
    grad_maps_weight = t_dot(maps_round, normed)
    grad_step_weight = t_dot(step_round, normed)
    inner_part, gate_sum = lax.optimization_barrier((grad_inner_weight.astype(BF16), gate_sum))
    inner_sum = reduce(inner_part)
    grad_gate_weight = gate_sum.astype(F32)

    partial = dot_t(gate_round, gate_weight) + dot_t(inner_round, inner_weight) + dot_t(step_round, step_weight)
    column = lax.axis_index("head") * local_width
    other_column = local_width - column
    own_part = lax.dynamic_slice_in_dim(partial, column, local_width, 1)
    other_part = lax.dynamic_slice_in_dim(partial, other_column, local_width, 1)
    input_share = own_part + swap(other_part.astype(BF16)).astype(F32)
    maps_rows = lax.dynamic_slice_in_dim(maps_weight, column, local_width, 0)
    input_share = input_share + dot_t(maps_round, maps_rows)
    normal_own = own_h.astype(F32) * inverse
    grad_normal = input_share * norm_gain.astype(F32)
    dot_sum = jnp.sum(grad_normal * normal_own, axis=-1, keepdims=True)
    dot_sum = dot_sum + swap(dot_sum)
    grad_hidden = inverse * (grad_normal - normal_own * (dot_sum / width_all)) + own_c.astype(F32)
    grad_norm_gain = jnp.sum(input_share * normal_own, axis=0)

    branch = dot(gated_norm, output_weight)
    own_branch = lax.dynamic_slice_in_dim(branch, column, local_width, 1)
    other_branch = lax.dynamic_slice_in_dim(branch, other_column, local_width, 1)
    output = own_h.astype(F32) + own_branch + swap(other_branch.astype(BF16)).astype(F32)

    misc = [grad_norm_gain, grad_maps_kernel.reshape(-1), grad_maps_bias[0], grad_step_bias, grad_decay_log, grad_skip_gain]
    used = sum(v.shape[0] for v in misc)
    misc_rows = -(-used // inner)
    misc.append(jnp.zeros((misc_rows * inner - used,), F32))
    small_rows = jnp.concatenate(
        [grad_maps_weight.reshape(-1, inner), grad_step_weight.reshape(-1, inner), grad_inner_kernel, grad_inner_bias, gate_gain_row,
         jnp.concatenate(misc).reshape(misc_rows, inner)], axis=0
    )
    small = reduce(small_rows)
    maps_end = 2 * state * width_all // inner
    weight_rows = maps_end + heads * width_all // inner
    at = weight_rows + taps
    tail_flat = small[at + 2 :].reshape(-1)
    ends = [0]
    for v in misc[:-1]:
        ends.append(ends[-1] + v.shape[0])
    tails = [tail_flat[ends[i] : ends[i + 1]] for i in range(len(misc) - 1)]
    shape = (seq_count, length, local_width)
    return (
        output.reshape(shape), grad_hidden.reshape(shape), tails[0], grad_gate_weight, inner_sum.astype(F32),
        small[maps_end:weight_rows].reshape(heads, width_all).T,
        small[:maps_end].reshape(2 * state, width_all).T, small[weight_rows:at], small[at],
        tails[1].reshape(maps_kernel.shape), tails[2], tails[3], tails[4], tails[5], small[at + 1], grad_output_weight,
    )


def solution(mesh):
    rows = P("batch", "seq", "head")
    cols = P(None, "head")
    vec = P("head")
    return jax.shard_map(
        on_device,
        mesh=mesh,
        in_specs=(rows, vec, cols, cols, cols, P(), cols, vec, P(), P(), vec, vec, vec, vec, P("head", None), rows),
        out_specs=(rows, rows, vec, cols, cols, cols, P(), cols, vec, P(), P(), vec, vec, vec, vec, P("head", None)),
        check_vma=False,
    )
```
